1024 devices in a mesh: row: 64 (over z, x), col: 16 (over y, core).
Axes of the slice: x: 4, y: 8, z: 16, core: 2. Of those that a mesh axis runs over, the one named last changes fastest.
Arguments:
- matrix: float32 [16384, 16384], P('row', 'col'), as said below
Outputs:
- factored: float32 [16384, 16384], P('row', 'col')
Inputs may be any that keep to these rules, and one draw needn't show every extreme that they name: `matrix`: each diagonal entry lies between 3 and 6 times the square root of 256; every other entry has magnitude 6 or less.
All inputs are finite; a program needn't handle non-finite values.
Results may differ from the reference program's by a relative error of at most 0.00085.
Values may be sent and summed in bfloat16 or wider, within the bound.
A program may use at most 32 MiB of HBM per device.

```python
import jax
import jax.numpy as jnp
from jax import lax

NB = 256
TICKS = 1
SWEEPS = 2
ORDER = 16384
N_COL = 16


def draw_matrix(key, part):
    keyed = jax.random.fold_in(key, 7)
    first_key, second_key = jax.random.split(keyed, 2)
    noise = jnp.clip(jax.random.normal(first_key, (ORDER, ORDER), jnp.float32), -6.0, 6.0)
    diagonal = jnp.exp(jax.random.uniform(second_key, (ORDER,), jnp.float32, jnp.log(3.0), jnp.log(6.0))) * jnp.sqrt(jnp.float32(NB))
    positions = jnp.arange(ORDER, dtype=jnp.int32)
    return noise.at[positions, positions].set(diagonal).astype(jnp.float32)


def setup_inputs(seed: int = 0) -> dict:
    keys = jax.random.split(jax.random.key(seed), 2)
    return {
        "matrix": draw_matrix(jax.random.fold_in(keys[1], 71), 0),
    }


def newton(square):
    size = square.shape[0]
    identity = jnp.eye(size, dtype=jnp.float32)
    approx = identity / jnp.diagonal(square)[None, :]
    for sweep in range(SWEEPS):
        product = jnp.dot(square, approx, precision=lax.Precision.HIGHEST)
        approx = jnp.dot(approx, 2.0 * identity - product, precision=lax.Precision.HIGHEST)
    return approx


def reference(matrix):
    width = ORDER // N_COL
    positions = jnp.arange(ORDER, dtype=jnp.int32)
    done = positions < 0
    current = matrix
    for tick in range(TICKS):
        first = tick * (width + NB)
        square = current[first:first + NB, first:first + NB]
        inverse = newton(square)
        done = done | ((positions >= first) & (positions < first + NB))
        lower = jnp.dot(current[:, first:first + NB], inverse, precision=lax.Precision.HIGHEST)
        lower = jnp.where(done[:, None], jnp.zeros_like(lower), lower).astype(jnp.bfloat16)
        upper_rows = current[first:first + NB, :]
        upper = jnp.where(done[None, :], jnp.zeros_like(upper_rows), upper_rows).astype(jnp.bfloat16)
        current = current - jnp.dot(lower, upper, preferred_element_type=jnp.float32)
    return current
```

```python
import functools

import jax
import jax.numpy as jnp
from jax import lax
from jax.experimental import pallas as pl
from jax.experimental.pallas import tpu as pltpu
from jax.sharding import PartitionSpec as P

NB = 256
NX = 4
NZ = 16
NY = 8
CHUNKS = 4
MESH = pl.DeviceIdType.MESH
HIGH = lax.Precision.HIGHEST
F32 = jnp.float32
BF16 = jnp.bfloat16


def inverse_of(square):
    size = square.shape[0]
    eye = lax.broadcasted_iota(jnp.int32, (size, size), 0) == lax.broadcasted_iota(
        jnp.int32, (size, size), 1
    )
    diagonal = jnp.where(eye, square, 0.0)
    across = 1.0 / jnp.sum(diagonal, axis=0, keepdims=True)
    down = 1.0 / jnp.sum(diagonal, axis=1, keepdims=True)
    identity = jnp.where(eye, 1.0, 0.0)
    error = identity - square * across
    first = identity + error
    second = jnp.dot(error, error, precision=HIGH, preferred_element_type=F32)
    third = jnp.dot(first, second, precision=HIGH, preferred_element_type=F32)
    return down * (first + third)


def kernel(m_hbm, l_ref, u_ref, m_buf, x_buf, m_sem, send_sem, own_sem, ux_sem, xz_sem, xx_sem,
           ly_sem, ls_sem, z_ready, y_ready):
    row, col = lax.axis_index("row"), lax.axis_index("col")
    z, x = row // NX, row % NX
    y, core = col // 2, col % 2
    rows, cols = u_ref.shape
    quarter = rows // NX
    chunk = quarter // CHUNKS
    piece = NB // NX
    half = rows // 2
    at_root_row = row == 0
    at_first_col = col == 0
    at_root = at_root_row & at_first_col

    def at_x(j):
        return z * NX + (x + j) % NX

    def at_z(k):
        return ((z + k) % NZ) * NX + x

    def at_y(k, c):
        return ((y + k) % NY) * 2 + c

    load = pltpu.make_async_copy(m_hbm, m_buf, m_sem)
    load.start()
    barrier = pltpu.get_barrier_semaphore()
    near = [(at_x(1), col), (at_x(2), col), (at_x(3), col), (at_z(1), col), (at_z(NZ - 1), col),
            (row, at_y(1, core)), (row, at_y(NY - 1, core)), (row, at_y(0, 1 - core))]
    for device in near:
        pl.semaphore_signal(barrier, inc=1, device_id=device, device_id_type=MESH)

    sent = []

    def send(cond, src, dst, recv, device):
        copy = pltpu.make_async_remote_copy(
            src_ref=src, dst_ref=dst, send_sem=send_sem.at[len(sent)], recv_sem=recv,
            device_id=device, device_id_type=MESH,
        )
        sent.append((cond, copy))

        @pl.when(cond)
        def _():
            copy.start()

    def arrived(ref, sem):
        pltpu.make_async_copy(ref, ref, sem).wait()

    load.wait()

    @pl.when(at_root_row)
    def _():
        columns = col * cols + lax.broadcasted_iota(jnp.int32, (rows, cols), 1)
        u_ref[...] = jnp.where(columns < NB, 0.0, m_buf[...]).astype(BF16)

    @pl.when(at_root)
    def _():
        x_buf[...] = inverse_of(m_buf[:, 0:NB])

    pl.semaphore_wait(barrier, len(near))

    @pl.when(core == 0)
    def _():
        @pl.when((y != 0) & (y != NY // 2) & (y != NY // 2 + 1))
        def _():
            pl.semaphore_wait(y_ready, 1)

        @pl.when((y > 0) & (y <= NY // 2))
        def _():
            pl.semaphore_signal(y_ready, 1, device_id=(row, at_y(NY - 1, 0)), device_id_type=MESH)

        @pl.when(y > NY // 2)
        def _():
            pl.semaphore_signal(y_ready, 1, device_id=(row, at_y(1, 0)), device_id_type=MESH)

    @pl.when(at_first_col)
    def _():
        @pl.when((z != 0) & (z != NZ // 2) & (z != NZ // 2 + 1))
        def _():
            pl.semaphore_wait(z_ready, 1)

        @pl.when((z > 0) & (z <= NZ // 2))
        def _():
            pl.semaphore_signal(z_ready, 1, device_id=(at_z(NZ - 1), col), device_id_type=MESH)

        @pl.when(z > NZ // 2)
        def _():
            pl.semaphore_signal(z_ready, 1, device_id=(at_z(1), col), device_id_type=MESH)

    def x_part(q):
        return x_buf.at[pl.ds(pl.multiple_of(q * piece, piece), piece), :]

    def u_part(q, k):
        return u_ref.at[pl.ds(pl.multiple_of(q * quarter + k * chunk, chunk), chunk), :]

    def u_quarter(q):
        return u_ref.at[pl.ds(pl.multiple_of(q * quarter, quarter), quarter), :]

    for q in (2, 1, 3):
        send(at_root, x_part(q), x_part(q), xz_sem, (q, col))
    for k in range(CHUNKS):
        for q in (2, 1, 3):
            send(at_root_row, u_part(q, k), u_part(q, k), own_sem.at[k], (q, col))

    def spread_u(cond):
        for k in range(CHUNKS):
            @pl.when(cond & (row != 0))
            def _():
                arrived(u_part(x, k), own_sem.at[k])

            part = u_part(x, k)
            send(cond & (z < NZ // 2), part, part, own_sem.at[k], (at_z(1), col))
            send(cond & ((z == 0) | (z > NZ // 2 + 1)), part, part, own_sem.at[k], (at_z(NZ - 1), col))
            for j in (2, 1, 3):
                send(cond & (at_x(j) != 0), part, part, ux_sem.at[j - 1], (at_x(j), col))

    def spread_x(cond):
        @pl.when(cond & (row != 0))
        def _():
            arrived(x_part(x), xz_sem)

        @pl.when(cond & (z == 0))
        def _():
            pl.semaphore_wait(z_ready, 2)

        for k in (8, 7, 9, 6, 10, 5, 11, 4, 12, 3, 13, 2, 14, 1, 15):
            send(cond & (z == 0), x_part(x), x_part(x), xz_sem, (at_z(k), col))
        for j in (2, 1, 3):
            send(cond & (at_x(j) != 0), x_part(x), x_part(x), xx_sem.at[j - 1], (at_x(j), col))

    x_first = (z == 0) | ((z > 4) & (z < 12))
    spread_x(at_first_col & x_first)
    spread_u(row >= 0)
    spread_x(at_first_col & jnp.logical_not(x_first))

    @pl.when(at_first_col & (row != 0))
    def _():
        for j in (1, 2, 3):
            arrived(x_part((x + NX - j) % NX), xx_sem.at[j - 1])

    @pl.when(at_first_col)
    def _():
        pl.semaphore_wait(y_ready, 2)

    for h in (0, 1):
        part = l_ref.at[pl.ds(h * half, half), :]

        @pl.when(at_first_col)
        def _():
            product = jnp.dot(m_buf[pl.ds(h * half, half), 0:NB], x_buf[...], precision=HIGH,
                              preferred_element_type=F32)
            l_ref[pl.ds(h * half, half), :] = jnp.where(at_root_row, 0.0, product).astype(BF16)

        for k in (4, 3, 5, 2, 6, 1, 7):
            send(at_first_col, part, part, ly_sem, (row, at_y(k, h)))
        send(at_first_col, part, part, ly_sem if h == 1 else ls_sem, (row, 1))

    mine = l_ref.at[pl.ds(pl.multiple_of(core * half, half), half), :]
    other = l_ref.at[pl.ds(pl.multiple_of((1 - core) * half, half), half), :]

    @pl.when(col != 0)
    def _():
        arrived(mine, ly_sem)

    send(y != 0, mine, mine, ls_sem, (row, at_y(0, 1 - core)))

    @pl.when(col != 0)
    def _():
        arrived(other, ls_sem)

    @pl.when(row != 0)
    def _():
        for j in (1, 2, 3):
            arrived(u_quarter((x + NX - j) % NX), ux_sem.at[j - 1])

    for cond, copy in sent:
        @pl.when(cond)
        def _(copy=copy):
            copy.wait_send()


def shards(matrix):
    rows, cols = matrix.shape
    sends = 3 + 3 * CHUNKS + 5 * CHUNKS + 2 * 18 + 16 + 1
    lower, upper = pl.pallas_call(
        kernel,
        out_shape=(jax.ShapeDtypeStruct((rows, NB), BF16), jax.ShapeDtypeStruct((rows, cols), BF16)),
        in_specs=[pl.BlockSpec(memory_space=pl.ANY)],
        out_specs=(pl.BlockSpec(memory_space=pltpu.VMEM), pl.BlockSpec(memory_space=pltpu.VMEM)),
        scratch_shapes=[
            pltpu.VMEM((rows, cols), F32),
            pltpu.VMEM((NB, NB), F32),
            pltpu.SemaphoreType.DMA,
            pltpu.SemaphoreType.DMA((sends,)),
            pltpu.SemaphoreType.DMA((CHUNKS,)),
            pltpu.SemaphoreType.DMA((3,)),
            pltpu.SemaphoreType.DMA,
            pltpu.SemaphoreType.DMA((3,)),
            pltpu.SemaphoreType.DMA,
            pltpu.SemaphoreType.DMA,
            pltpu.SemaphoreType.REGULAR,
            pltpu.SemaphoreType.REGULAR,
        ],
        compiler_params=pltpu.CompilerParams(collective_id=0, has_side_effects=True),
    )(matrix)
    return matrix - jnp.dot(lower, upper, preferred_element_type=F32)


def solution(mesh):
    return jax.shard_map(
        shards,
        mesh=mesh,
        in_specs=(P("row", "col"),),
        out_specs=P("row", "col"),
        check_vma=False,
    )
```

```python
import jax
import jax.numpy as jnp
from jax import lax
from jax.experimental import pallas as pl
from jax.experimental.pallas import tpu as pltpu
from jax.sharding import PartitionSpec as P

NB = 256
NX = 4
NZ = 16
NY = 8
CHUNKS = 4
MESH = pl.DeviceIdType.MESH
F32 = jnp.float32
BF16 = jnp.bfloat16


def split(a):
    high = a.astype(BF16)
    return high, (a - high.astype(F32)).astype(BF16)


def product(a, b):
    (ah, al), (bh, bl) = a, b
    dot = lambda u, v: jnp.dot(u, v, preferred_element_type=F32)
    return dot(ah, bh) + (dot(ah, bl) + dot(al, bh))


def inverse_of(square):
    size = square.shape[0]
    eye = lax.broadcasted_iota(jnp.int32, (size, size), 0) == lax.broadcasted_iota(
        jnp.int32, (size, size), 1
    )
    diagonal = jnp.where(eye, square, 0.0)
    across = 1.0 / jnp.sum(diagonal, axis=0, keepdims=True)
    down = 1.0 / jnp.sum(diagonal, axis=1, keepdims=True)
    identity = jnp.where(eye, 1.0, 0.0)
    error = identity - square * across
    first = identity + error
    parts = split(error)
    second = product(parts, parts)
    return down * (first + (second + product(parts, split(second))))


def kernel(m_ref, l_ref, u_ref, c_buf, parts, x_buf, send_sem, own_sem, ux_sem, mc_sem,
           xz_sem, xx_sem, ly_sem, ls_sem):
    row, col = lax.axis_index("row"), lax.axis_index("col")
    z, x = lax.div(row, NX), lax.rem(row, NX)
    y, core = lax.div(col, 2), lax.rem(col, 2)
    rows, cols = u_ref.shape
    quarter = rows // NX
    chunk = quarter // CHUNKS
    piece = NB // NX
    half = NB // 2
    top = row == 0
    plane = y == 0
    first_col = col == 0
    root = top & first_col

    plus = z <= NZ // 2
    away = jnp.where(plus, z, NZ - z)
    parent = jnp.where(
        plane, lax.div(jnp.maximum(away - 1, 0), 4) * 4, lax.div(jnp.maximum(away - 1, 0), 3) * 3
    )
    parent_z = jnp.where(plus, parent, lax.rem(NZ - parent, NZ))
    relay = jnp.where(plane, lax.rem(away, 4), lax.rem(away, 3)) == 0
    step = jnp.where(plane, 4, 3)

    def down_z(j):
        far = relay & (j <= step)
        return [
            (far & plus & (away + j <= NZ // 2), lax.rem(z + j, NZ)),
            (far & (jnp.logical_not(plus) | (z == 0)) & (away + j < NZ // 2), lax.rem(z + NZ - j, NZ)),
        ]

    children = sum(jnp.where(c, 1, 0) for j in (4, 3, 2, 1) for c, _ in down_z(j))

    def at_x(j):
        return z * NX + lax.rem(x + j, NX)

    barrier = pltpu.get_barrier_semaphore()

    def greet(device):
        pl.semaphore_signal(barrier, inc=1, device_id=device, device_id_type=MESH)

    for j in (1, 2, 3):
        greet((at_x(j), col))
    greet((row, y * 2 + 1 - core))

    @pl.when(z != 0)
    def _():
        greet((parent_z * NX + x, col))

    @pl.when((z == 0) & (x != 0) & (col == 1))
    def _():
        greet((0, 0))

    @pl.when(y != 0)
    def _():
        greet((row, core))

    sent = []

    def send(cond, src, dst, recv, device):
        copy = pltpu.make_async_remote_copy(
            src_ref=src, dst_ref=dst, send_sem=send_sem.at[len(sent)], recv_sem=recv,
            device_id=device, device_id_type=MESH,
        )
        sent.append((cond, copy))

        @pl.when(cond)
        def _():
            copy.start()

    def arrived(ref, sem):
        pltpu.make_async_copy(ref, ref, sem).wait()

    @pl.when(top)
    def _():
        columns = col * cols + lax.broadcasted_iota(jnp.int32, (rows, cols), 1)
        u_ref[...] = jnp.where(columns < NB, 0.0, m_ref[...]).astype(BF16)

    @pl.when(root)
    def _():
        inverse = inverse_of(m_ref[:, :NB])
        x_buf[0] = inverse[:, :half]
        x_buf[1] = inverse[:, half:]

    pl.semaphore_wait(
        barrier, 4 + children + jnp.where(plane, NY - 1, 0) + jnp.where(root, NX - 1, 0)
    )

    def x_part(h, q):
        return x_buf.at[h, pl.ds(pl.multiple_of(q * piece, piece), piece), :]

    def u_part(q, k):
        return u_ref.at[pl.ds(pl.multiple_of(q * quarter + k * chunk, chunk), chunk), :]

    def u_quarter(q):
        return u_ref.at[pl.ds(pl.multiple_of(q * quarter, quarter), quarter), :]

    send(root, x_part(1, 0), x_part(1, 0), xz_sem, (0, 1))
    for q in (2, 1, 3):
        for h in (1, 0):
            send(root, x_part(h, q), x_part(h, q), xz_sem, (q, h))
    for k in range(CHUNKS):
        for q in (2, 1, 3):
            send(top, u_part(q, k), u_part(q, k), own_sem.at[k], (q, col))
    send(first_col, m_ref.at[:, pl.ds(0, NB)], c_buf, mc_sem, (row, 1))

    @pl.when(plane & jnp.logical_not(root))
    def _():
        arrived(x_part(core, x), xz_sem)

    mine = x_part(core, x)
    for j in (4, 3, 2, 1):
        for cond, to in down_z(j):
            send(plane & cond, mine, mine, xz_sem, (to * NX + x, col))
    for j in (2, 1, 3):
        send(plane & (at_x(j) != 0), mine, mine, xx_sem.at[j - 1], (at_x(j), col))

    def spread(cond, down):
        for k in range(CHUNKS):
            part = u_part(x, k)

            @pl.when(cond & jnp.logical_not(top))
            def _():
                arrived(part, own_sem.at[k])

            if down:
                for j in (4, 3, 2, 1):
                    for further, to in down_z(j):
                        send(cond & further, part, part, own_sem.at[k], (to * NX + x, col))
            for j in (2, 1, 3):
                send(cond & (at_x(j) != 0), part, part, ux_sem.at[j - 1], (at_x(j), col))

    spread(relay, True)

    @pl.when(first_col)
    def _():
        parts[0], parts[1] = split(m_ref[:, :NB])

    @pl.when(col == 1)
    def _():
        arrived(c_buf, mc_sem)
        parts[0], parts[1] = split(c_buf[...])

    own = pl.ds(pl.multiple_of(core * half, half), half)
    other = pl.ds(pl.multiple_of((1 - core) * half, half), half)

    @pl.when(plane & jnp.logical_not(top))
    def _():
        for j in (1, 2, 3):
            arrived(x_part(core, lax.rem(x + NX - j, NX)), xx_sem.at[j - 1])
        l_ref[:, own] = product((parts[0], parts[1]), split(x_buf[core])).astype(BF16)

    @pl.when(plane & top)
    def _():
        l_ref[:, own] = jnp.zeros((rows, half), BF16)

    for k in (4, 3, 5, 2, 6, 1, 7):
        send(plane, l_ref.at[:, own], l_ref.at[:, own], ly_sem, (row, k * 2 + core))

    spread(jnp.logical_not(relay), False)

    @pl.when(jnp.logical_not(plane))
    def _():
        arrived(l_ref.at[:, own], ly_sem)

    send(row >= 0, l_ref.at[:, own], l_ref.at[:, own], ls_sem, (row, y * 2 + 1 - core))

    @pl.when(row != 0)
    def _():
        for j in (1, 2, 3):
            arrived(u_quarter(lax.rem(x + NX - j, NX)), ux_sem.at[j - 1])

    arrived(l_ref.at[:, other], ls_sem)

    @pl.when(plane & top & (x != 0))
    def _():
        for j in (1, 2, 3):
            arrived(x_part(core, lax.rem(x + NX - j, NX)), xx_sem.at[j - 1])

    for cond, copy in sent:
        @pl.when(cond)
        def _(copy=copy):
            copy.wait_send()


def shards(matrix):
    rows, cols = matrix.shape
    lower, upper = pl.pallas_call(
        kernel,
        out_shape=(jax.ShapeDtypeStruct((rows, NB), BF16), jax.ShapeDtypeStruct((rows, cols), BF16)),
        in_specs=[pl.BlockSpec(memory_space=pltpu.VMEM)],
        out_specs=(pl.BlockSpec(memory_space=pltpu.VMEM), pl.BlockSpec(memory_space=pltpu.VMEM)),
        scratch_shapes=[
            pltpu.VMEM((rows, NB), F32),
            pltpu.VMEM((2, rows, NB), BF16),
            pltpu.VMEM((2, NB, NB // 2), F32),
            pltpu.SemaphoreType.DMA((128,)),
            pltpu.SemaphoreType.DMA((CHUNKS,)),
            pltpu.SemaphoreType.DMA((3,)),
            pltpu.SemaphoreType.DMA,
            pltpu.SemaphoreType.DMA,
            pltpu.SemaphoreType.DMA((3,)),
            pltpu.SemaphoreType.DMA,
            pltpu.SemaphoreType.DMA,
        ],
        compiler_params=pltpu.CompilerParams(
            collective_id=0, has_side_effects=True, vmem_limit_bytes=24 * 1024 * 1024
        ),
    )(matrix)
    return matrix - jnp.dot(lower, upper, preferred_element_type=F32)


def solution(mesh):
    return jax.shard_map(
        shards,
        mesh=mesh,
        in_specs=(P("row", "col"),),
        out_specs=P("row", "col"),
        check_vma=False,
    )
```

```python
import jax
import jax.numpy as jnp
from jax import lax
from jax.experimental import pallas as pl
from jax.experimental.pallas import tpu as pltpu
from jax.sharding import PartitionSpec as P

NB = 256
NX = 4
NZ = 16
NY = 8
CHAIN = 8
HUB = 13
CHUNKS = 4
MESH = pl.DeviceIdType.MESH
F32 = jnp.float32
BF16 = jnp.bfloat16


def split(a):
    high = a.astype(BF16)
    return high, (a - high.astype(F32)).astype(BF16)


def product(a, b):
    (ah, al), (bh, bl) = a, b
    dot = lambda u, v: jnp.dot(u, v, preferred_element_type=F32)
    return dot(ah, bh) + (dot(ah, bl) + dot(al, bh))


def inverse_of(square):
    size = square.shape[0]
    eye = lax.broadcasted_iota(jnp.int32, (size, size), 0) == lax.broadcasted_iota(
        jnp.int32, (size, size), 1
    )
    diagonal = jnp.where(eye, square, 0.0)
    across = 1.0 / jnp.sum(diagonal, axis=0, keepdims=True)
    down = 1.0 / jnp.sum(diagonal, axis=1, keepdims=True)
    identity = jnp.where(eye, 1.0, 0.0)
    error = identity - square * across
    first = identity + error
    parts = split(error)
    second = product(parts, parts)
    return down * (first + (second + product(parts, split(second))))


def kernel(m_ref, l_ref, u_ref, x_buf, send_sem, own_sem, ux_sem, xz_sem, xx_sem, ly_sem, ls_sem,
           ready_x, ready_y, ready_z, ready_w, ready_v):
    row, col = lax.axis_index("row"), lax.axis_index("col")
    z, x = lax.div(row, NX), lax.rem(row, NX)
    y, core = lax.div(col, 2), lax.rem(col, 2)
    rows, cols = u_ref.shape
    quarter = rows // NX
    chunk = quarter // CHUNKS
    piece = NB // NX
    half = NB // 2
    top = row == 0
    below = row != 0
    first_col = col == 0
    other_col = col != 0
    root = top & first_col
    bottom = z == 0
    one = lambda cond: jnp.where(cond, 1, 0)

    hub = z == HUB
    chain = (z < CHAIN) & (lax.rem(z, 2) == 0)
    beyond = [(hub, HUB + j) for j in (-1, 1, -2, 2, -3, -4)]
    down_u = [(chain, z + 2), (chain, z + 1)] + beyond
    step = first_col & ((z == 0) | (z == 4))
    down_x = [(step, z + j) for j in (1, 2, 3, 4)] + [(first_col & hub, to) for _, to in beyond]
    extra = [(step, z + 3), (step, z + 4)]
    parent_z = jnp.where(z > CHAIN, HUB, jnp.where(lax.rem(z, 2) == 0, z - 2, z - 1))
    second_parent = first_col & ((z == 3) | (z == 4) | (z == 7) | (z == 8))
    second_z = jnp.where(z < 5, 0, 4)

    def at_x(j):
        return z * NX + lax.rem(x + j, NX)

    from_root_x = bottom & (x != 0) & first_col
    from_root_z = (z > 0) & (z < 5) & (x == 0) & first_col
    by_parent = (z > 2) | ((z > 0) & jnp.logical_not(from_root_z))
    by_second = second_parent & jnp.logical_not(from_root_z)

    barrier = pltpu.get_barrier_semaphore()

    def signal(cond, sem, device):
        @pl.when(cond)
        def _():
            pl.semaphore_signal(sem, inc=1, device_id=device, device_id_type=MESH)

    usual = jnp.logical_not(root)
    signal(from_root_x | from_root_z, barrier, (0, 0))
    signal(row >= 0, barrier, (row, y * 2 + 1 - core))
    for j in (1, 2, 3):
        signal(usual & (x + j < NX), barrier, (row + j, col))
    for cond, to in down_u + extra:
        signal(usual & cond, barrier, (to * NX + x, col))
    signal(bottom, barrier, (HUB * NX + x, col))
    for k in range(2, 2 * NY):
        signal(below & first_col, barrier, (row, k))
    signal(below & (y == 2), barrier, (row, 8 + core))

    pl.semaphore_wait(
        barrier,
        jnp.where(root, 1 + NX - 1 + 4,
                  1 + x - one(from_root_x) + one(by_parent) + one(by_second)
                  + one(below & (y != 0)) + one(below & (y == 4))),
    )

    for j in (1, 2, 3):
        signal((x >= j) & jnp.logical_not(from_root_x & (x == j)), ready_x, (row - j, col))
    signal(by_parent & jnp.logical_not(hub), ready_z, (parent_z * NX + x, col))
    signal(by_second, ready_z, (second_z * NX + x, col))
    signal(hub, ready_w, (x, col))
    signal(below & (y != 0), ready_y, (row, 0))
    signal(below & (y == 4), ready_v, (row, 4 + core))

    sent = []

    def send(cond, part, recv, device):
        copy = pltpu.make_async_remote_copy(
            src_ref=part, dst_ref=part, send_sem=send_sem.at[len(sent)], recv_sem=recv,
            device_id=device, device_id_type=MESH,
        )
        sent.append((cond, copy))

        @pl.when(cond)
        def _():
            copy.start()

    def arrived(ref, sem):
        pltpu.make_async_copy(ref, ref, sem).wait()

    def wait_for(cond, sem, count):
        @pl.when(cond)
        def _():
            pl.semaphore_wait(sem, count)

    def x_part(q):
        return x_buf.at[pl.ds(pl.multiple_of(q * piece, piece), piece), :]

    def u_part(q, k, first):
        return u_ref.at[
            pl.ds(pl.multiple_of(q * quarter + k * chunk, chunk), chunk), pl.ds(first, cols - first)
        ]

    def u_quarter(q, first):
        return u_ref.at[pl.ds(pl.multiple_of(q * quarter, quarter), quarter), pl.ds(first, cols - first)]

    def scatter_u(cond, first):
        for k in range(CHUNKS):
            for q in (2, 1, 3):
                send(cond, u_part(q, k, first), own_sem.at[k], (q, col))

    def spread_u(cond, first):
        for k in range(CHUNKS):
            part = u_part(x, k, first)

            @pl.when(cond & below)
            def _():
                arrived(part, own_sem.at[k])

            for j in (2, 1, 3):
                send(cond & (at_x(j) != 0), part, ux_sem.at[j - 1], (at_x(j), col))
            for further, to in down_u:
                send(cond & further, part, own_sem.at[k], (to * NX + x, col))

    def late_u(cond, first):
        for k in range(CHUNKS):
            send(cond & bottom, u_part(x, k, first), own_sem.at[k], (HUB * NX + x, col))

    @pl.when(root)
    def _():
        x_buf[...] = inverse_of(m_ref[:, :NB])

    for q in (2, 1, 3):
        send(root, x_part(q), xz_sem, (q, 0))

    @pl.when(top)
    def _():
        columns = col * cols + lax.broadcasted_iota(jnp.int32, (rows, cols), 1)
        u_ref[...] = jnp.where(columns < NB, 0.0, m_ref[...]).astype(BF16)
        l_ref[...] = jnp.zeros((rows, NB), BF16)

    @pl.when(first_col & below)
    def _():
        u_ref[:, :NB] = jnp.zeros((rows, NB), BF16)

    wait_for(usual & (x != NX - 1), ready_x, NX - 1 - x)
    scatter_u(top & other_col, 0)
    wait_for(usual & (chain | hub), ready_z, jnp.where(hub, 6, jnp.where(step, 4, 2)))
    spread_u(other_col, 0)
    wait_for(bottom & other_col, ready_w, 1)
    late_u(other_col, 0)

    @pl.when(first_col & below)
    def _():
        arrived(x_part(x), xz_sem)

    mine = x_part(x)
    for j in (2, 1, 3):
        send(first_col & (at_x(j) != 0), mine, xx_sem.at[j - 1], (at_x(j), 0))
    for cond, to in down_x:
        send(cond, mine, xz_sem, (to * NX + x, 0))
    scatter_u(root, NB)
    wait_for(bottom & first_col, ready_w, 1)
    send(bottom & first_col, mine, xz_sem, (HUB * NX + x, 0))

    @pl.when(first_col & below)
    def _():
        left = split(m_ref[:, :NB])
        for j in (1, 2, 3):
            arrived(x_part(lax.rem(x + NX - j, NX)), xx_sem.at[j - 1])
        l_ref[...] = product(left, split(x_buf[...])).astype(BF16)
        pl.semaphore_wait(ready_y, 2 * NY - 2)

    def l_part(h):
        return l_ref.at[pl.ds(pl.multiple_of(h * half, half), half), :]

    for k in (2, 6, 3, 7, 1, 5):
        for h in (0, 1):
            send(first_col & below, l_part(h), ly_sem, (row, k * 2 + h))
    send(first_col & below, l_ref, ly_sem, (row, 1))

    spread_u(first_col, NB)
    late_u(first_col, NB)

    @pl.when(below & (y != 0))
    def _():
        arrived(l_part(core), ly_sem)

    wait_for(below & (y == 2), ready_v, 1)
    send(below & (y == 2), l_part(core), ly_sem, (row, 8 + core))
    send(below & (y != 0), l_part(core), ls_sem, (row, y * 2 + 1 - core))

    for cond, first in ((other_col, 0), (first_col, NB)):
        @pl.when(cond & below)
        def _():
            for j in (1, 2, 3):
                arrived(u_quarter(lax.rem(x + NX - j, NX), first), ux_sem.at[j - 1])

    @pl.when(below & (y != 0))
    def _():
        arrived(l_part(1 - core), ls_sem)

    @pl.when(below & (col == 1))
    def _():
        arrived(l_ref, ly_sem)

    for cond, copy in sent:
        @pl.when(cond)
        def _(copy=copy):
            copy.wait_send()


def shards(matrix):
    rows, cols = matrix.shape
    lower, upper = pl.pallas_call(
        kernel,
        out_shape=(jax.ShapeDtypeStruct((rows, NB), BF16), jax.ShapeDtypeStruct((rows, cols), BF16)),
        in_specs=[pl.BlockSpec(memory_space=pltpu.VMEM)],
        out_specs=(pl.BlockSpec(memory_space=pltpu.VMEM), pl.BlockSpec(memory_space=pltpu.VMEM)),
        scratch_shapes=[
            pltpu.VMEM((NB, NB), F32),
            pltpu.SemaphoreType.DMA((160,)),
            pltpu.SemaphoreType.DMA((CHUNKS,)),
            pltpu.SemaphoreType.DMA((3,)),
            pltpu.SemaphoreType.DMA,
            pltpu.SemaphoreType.DMA((3,)),
            pltpu.SemaphoreType.DMA,
            pltpu.SemaphoreType.DMA,
        ]
        + [pltpu.SemaphoreType.REGULAR] * 5,
        compiler_params=pltpu.CompilerParams(
            collective_id=0, has_side_effects=True, vmem_limit_bytes=24 * 1024 * 1024
        ),
    )(matrix)
    return matrix - jnp.dot(lower, upper, preferred_element_type=F32)


def solution(mesh):
    return jax.shard_map(
        shards,
        mesh=mesh,
        in_specs=(P("row", "col"),),
        out_specs=P("row", "col"),
        check_vma=False,
    )
```

```python
import jax
import jax.numpy as jnp
from jax import lax
from jax.experimental import pallas as pl
from jax.experimental.pallas import tpu as pltpu
from jax.sharding import PartitionSpec as P

NB = 256
NX = 4
NZ = 16
NY = 8
CHAIN = 8
HUB = 13
NEAR = 6
CHUNKS = 4
MESH = pl.DeviceIdType.MESH
F32 = jnp.float32
BF16 = jnp.bfloat16


def split(a):
    high = a.astype(BF16)
    return high, (a - high.astype(F32)).astype(BF16)


def product(a, b):
    (ah, al), (bh, bl) = a, b
    dot = lambda u, v: jnp.dot(u, v, preferred_element_type=F32)
    return dot(ah, bh) + (dot(ah, bl) + dot(al, bh))


def inverse_of(square):
    size = square.shape[0]
    eye = lax.broadcasted_iota(jnp.int32, (size, size), 0) == lax.broadcasted_iota(
        jnp.int32, (size, size), 1
    )
    diagonal = jnp.where(eye, square, 0.0)
    across = 1.0 / jnp.sum(diagonal, axis=0, keepdims=True)
    down = 1.0 / jnp.sum(diagonal, axis=1, keepdims=True)
    identity = jnp.where(eye, 1.0, 0.0)
    error = identity - square * across
    first = identity + error
    parts = split(error)
    second = product(parts, parts)
    return down * (first + (second + product(parts, split(second))))


def kernel(m_hbm, l_ref, u_ref, m_ref, x_buf, m_sem, send_sem, own_sem, ux_sem, xz_sem, xx_sem, ly_sem, ls_sem,
           ready_x, ready_y, ready_z, ready_w, ready_v):
    row, col = lax.axis_index("row"), lax.axis_index("col")
    z, x = lax.div(row, NX), lax.rem(row, NX)
    y, core = lax.div(col, 2), lax.rem(col, 2)
    rows, cols = u_ref.shape
    quarter = rows // NX
    chunk = quarter // CHUNKS
    piece = NB // NX
    half = NB // 2
    top = row == 0
    below = row != 0
    first_col = col == 0
    other_col = col != 0
    root = top & first_col
    bottom = z == 0
    one = lambda cond: jnp.where(cond, 1, 0)

    hub = z == HUB
    chain = other_col & (z <= CHAIN) & (lax.rem(z, 2) == 0)
    source = first_col & bottom
    relay = first_col & (z == 4)
    first_hub = first_col & hub
    other_hub = other_col & hub
    down_u = [(chain, z + 2), (chain, z + 1)] + [(other_hub, to) for to in (12, 14, 11, 15)]
    down_x = (
        [(source, to) for to in range(1, NEAR + 1)] + [(relay, 7), (relay, 8)]
        + [(first_hub, to) for to in (9, 14, 10, 15, 11, 12)]
    )
    parent_z = jnp.where(
        first_col,
        jnp.where(z <= NEAR, 0, jnp.where(z < 9, 4, HUB)),
        jnp.where(z > CHAIN + 2, HUB, jnp.where(lax.rem(z, 2) == 0, z - 2, z - 1)),
    )
    children = (jnp.where(source, NEAR, 0) + jnp.where(relay, 2, 0) + jnp.where(first_hub, 6, 0)
                + jnp.where(chain, 2, 0) + jnp.where(other_hub, 4, 0))

    def at_x(j):
        return z * NX + lax.rem(x + j, NX)

    from_root_x = bottom & (x != 0) & first_col
    from_root_z = (z > 0) & (z <= NEAR) & (x == 0) & first_col
    by_parent = (z > 0) & jnp.logical_not(from_root_z)

    narrow = pltpu.make_async_copy(m_hbm.at[:, pl.ds(0, NB)], m_ref.at[:, pl.ds(0, NB)], m_sem.at[0])
    rest = pl.ds(NB, cols - NB)
    wide = pltpu.make_async_copy(m_hbm.at[:, rest], m_ref.at[:, rest], m_sem.at[1])

    @pl.when(first_col | top)
    def _():
        narrow.start()

    @pl.when(top)
    def _():
        wide.start()

    barrier = pltpu.get_barrier_semaphore()

    usual = jnp.logical_not(root)

    def signal(cond, sem, device):
        one_more = lambda: pl.semaphore_signal(sem, inc=1, device_id=device, device_id_type=MESH)
        one_more() if cond is None else pl.when(cond)(one_more)

    paired = below | (y != 0)
    signal(paired, barrier, (row, y * 2 + 1 - core))
    signal((row == 1) & (col == 1), barrier, (0, 1))
    signal(bottom, barrier, (HUB * NX + x, col))

    @pl.when(usual)
    def _():
        signal(from_root_x | from_root_z, barrier, (0, 0))
        for j in (1, 2, 3):
            signal(x + j < NX, barrier, (row + j, col))
        for cond, to in down_u + down_x:
            signal(cond, barrier, (to * NX + x, col))

    @pl.when(below & first_col)
    def _():
        for k in range(2, 2 * NY):
            signal(None, barrier, (row, k))

    signal(below & (y == 2), barrier, (row, 8 + core))

    pl.semaphore_wait(
        barrier,
        jnp.where(root, NX - 1 + NEAR,
                  one(paired) + one(top & (col == 1)) + x - one(from_root_x) + one(by_parent)
                  + one(below & (y != 0)) + one(below & (y == 4))),
    )

    @pl.when(usual)
    def _():
        for j in (1, 2, 3):
            signal((x >= j) & jnp.logical_not(from_root_x & (x == j)), ready_x, (row - j, col))
        signal(by_parent & jnp.logical_not(hub), ready_z, (parent_z * NX + x, col))
        signal(hub, ready_w, (x, col))
        signal(below & (y != 0), ready_y, (row, 0))
        signal(below & (y == 4), ready_v, (row, 4 + core))

    sections = []
    used = [0]

    def section(cond, body):
        group = []

        def send(part, recv, device, only=None):
            spot = used[0]
            used[0] += 1

            def begin():
                ref = part()
                pltpu.make_async_remote_copy(
                    src_ref=ref, dst_ref=ref, send_sem=send_sem.at[spot], recv_sem=recv,
                    device_id=device, device_id_type=MESH,
                ).start()

            group.append((only, part, spot))
            begin() if only is None else pl.when(only)(begin)

        pl.when(cond)(lambda: body(send))
        sections.append((cond, group))

    def arrived(ref, sem):
        pltpu.make_async_copy(ref, ref, sem).wait()

    def wait_for(cond, sem, count):
        @pl.when(cond)
        def _():
            pl.semaphore_wait(sem, count)

    def x_part(q):
        return x_buf.at[pl.ds(pl.multiple_of(q * piece, piece), piece), :]

    def u_part(q, k, first):
        return u_ref.at[
            pl.ds(pl.multiple_of(q * quarter + k * chunk, chunk), chunk), pl.ds(first, cols - first)
        ]

    def u_quarter(q, first):
        return u_ref.at[pl.ds(pl.multiple_of(q * quarter, quarter), quarter), pl.ds(first, cols - first)]

    def first_part(q, k):
        rows_here = pl.ds(pl.multiple_of(q * quarter + k * (quarter // 2), quarter // 2), quarter // 2)
        return u_ref.at[rows_here, pl.ds(NB, cols - NB)]

    def scatter_u(first):
        def body(send):
            for k in range(CHUNKS):
                for q in (2, 1, 3):
                    send(lambda q=q, k=k: u_part(q, k, first), own_sem.at[k], (q, col))
        return body

    not_back = [at_x(j) != 0 for j in (1, 2, 3)]

    def spread_u(first):
        def body(send):
            for k in range(CHUNKS):
                part = lambda k=k: u_part(x, k, first)

                @pl.when(below)
                def _():
                    arrived(part(), own_sem.at[k])

                for j in (2, 1, 3):
                    send(part, ux_sem.at[j - 1], (at_x(j), col), not_back[j - 1])
                for further, to in down_u:
                    send(part, own_sem.at[k], (to * NX + x, col), further)
        return body

    def late_u(first):
        def body(send):
            for k in range(CHUNKS):
                send(lambda k=k: u_part(x, k, first), own_sem.at[k], (HUB * NX + x, col))
        return body

    @pl.when(first_col | top)
    def _():
        narrow.wait()

    def start(send):
        x_buf[...] = inverse_of(m_ref[:, :NB])
        for q in (2, 1, 3):
            send(lambda q=q: x_part(q), xz_sem, (q, 0))

    section(root, start)

    @pl.when(top)
    def _():
        wide.wait()
        columns = col * cols + lax.broadcasted_iota(jnp.int32, (rows, cols), 1)
        u_ref[...] = jnp.where(columns < NB, 0.0, m_ref[...]).astype(BF16)
        l_ref[...] = jnp.zeros((rows, NB), BF16)

    wait_for(usual & (x != NX - 1), ready_x, NX - 1 - x)
    wait_for(usual & (children > 0), ready_z, children)

    section(top & other_col, scatter_u(0))
    section(other_col, spread_u(0))

    def last(first):
        def body(send):
            pl.semaphore_wait(ready_w, 1)
            late_u(first)(send)
        return body

    section(bottom & other_col, last(0))

    def inverse_rows(send):
        @pl.when(below)
        def _():
            u_ref[:, :NB] = jnp.zeros((rows, NB), BF16)
            arrived(x_part(x), xz_sem)

        mine = lambda: x_part(x)
        for j in (2, 1, 3):
            send(mine, xx_sem.at[j - 1], (at_x(j), 0), not_back[j - 1])
        for cond, to in down_x:
            send(mine, xz_sem, (to * NX + x, 0), cond)

    section(first_col, inverse_rows)

    def scatter_first(send):
        for k in range(2):
            for q in (2, 1, 3):
                send(lambda q=q, k=k: first_part(q, k), own_sem.at[k], (q, col))

    section(root, scatter_first)

    def to_hub(send):
        pl.semaphore_wait(ready_w, 1)
        send(lambda: x_part(x), xz_sem, (HUB * NX + x, 0))

    section(first_col & bottom, to_hub)

    def l_part(h):
        return l_ref.at[pl.ds(pl.multiple_of(h * half, half), half), :]

    def make_lower(send):
        left = split(m_ref[:, :NB])
        for j in (1, 2, 3):
            arrived(x_part(lax.rem(x + NX - j, NX)), xx_sem.at[j - 1])
        l_ref[...] = product(left, split(x_buf[...])).astype(BF16)
        pl.semaphore_wait(ready_y, 2 * NY - 2)
        for k in (2, 6, 3, 7, 1, 5):
            for h in (0, 1):
                send(lambda h=h: l_part(h), ly_sem, (row, k * 2 + h))
        send(lambda: l_ref, ly_sem, (row, 1))

    section(first_col & below, make_lower)

    def spread_first(send):
        for k in range(2):
            @pl.when(below)
            def _():
                arrived(first_part(x, k), own_sem.at[k])

            for j in (2, 1, 3):
                send(lambda k=k: first_part(x, k), ux_sem.at[j - 1], (at_x(j), col), not_back[j - 1])
        for cond, to in down_x + [(bottom, HUB)]:
            for k in range(2):
                send(lambda k=k: first_part(x, k), own_sem.at[k], (to * NX + x, col), cond)

    section(first_col, spread_first)

    passes = y == 2

    def relay_lower(send):
        arrived(l_part(core), ly_sem)

        @pl.when(passes)
        def _():
            pl.semaphore_wait(ready_v, 1)

        send(lambda: l_part(core), ly_sem, (row, 8 + core), passes)
        send(lambda: l_part(core), ls_sem, (row, y * 2 + 1 - core))

    section(below & (y != 0), relay_lower)

    def finish(first):
        for j in (1, 2, 3):
            arrived(u_quarter(lax.rem(x + NX - j, NX), first), ux_sem.at[j - 1])

    pl.when(below & other_col)(lambda: finish(0))
    pl.when(below & first_col)(lambda: finish(NB))

    @pl.when(below & (y != 0))
    def _():
        arrived(l_part(1 - core), ls_sem)

    @pl.when(below & (col == 1))
    def _():
        arrived(l_ref, ly_sem)

    def sent(group):
        for only, part, spot in group:
            gone = lambda part=part, spot=spot: arrived(part(), send_sem.at[spot])
            gone() if only is None else pl.when(only)(gone)

    for cond, group in sections:
        pl.when(cond)(lambda group=group: sent(group))


def shards(matrix):
    rows, cols = matrix.shape
    lower, upper = pl.pallas_call(
        kernel,
        out_shape=(jax.ShapeDtypeStruct((rows, NB), BF16), jax.ShapeDtypeStruct((rows, cols), BF16)),
        in_specs=[pl.BlockSpec(memory_space=pl.ANY)],
        out_specs=(pl.BlockSpec(memory_space=pltpu.VMEM), pl.BlockSpec(memory_space=pltpu.VMEM)),
        scratch_shapes=[
            pltpu.VMEM((rows, cols), F32),
            pltpu.VMEM((NB, NB), F32),
            pltpu.SemaphoreType.DMA((2,)),
            pltpu.SemaphoreType.DMA((200,)),
            pltpu.SemaphoreType.DMA((CHUNKS,)),
            pltpu.SemaphoreType.DMA((3,)),
            pltpu.SemaphoreType.DMA,
            pltpu.SemaphoreType.DMA((3,)),
            pltpu.SemaphoreType.DMA,
            pltpu.SemaphoreType.DMA,
        ]
        + [pltpu.SemaphoreType.REGULAR] * 5,
        compiler_params=pltpu.CompilerParams(
            collective_id=0, has_side_effects=True, vmem_limit_bytes=24 * 1024 * 1024
        ),
    )(pltpu.with_memory_space_constraint(matrix, pltpu.HBM))
    return matrix - jnp.dot(lower, upper, preferred_element_type=F32)


def solution(mesh):
    return jax.shard_map(
        shards,
        mesh=mesh,
        in_specs=(P("row", "col"),),
        out_specs=P("row", "col"),
        check_vma=False,
    )
```

```python
import jax
import jax.numpy as jnp
from jax import lax
from jax.experimental import pallas as pl
from jax.experimental.pallas import tpu as pltpu
from jax.sharding import PartitionSpec as P

NB = 256
NX = 4
NZ = 16
NY = 8
CHAIN = 8
HUB = 13
NEAR = 6
CHUNKS = 4
MESH = pl.DeviceIdType.MESH
F32 = jnp.float32
BF16 = jnp.bfloat16


def split(a):
    high = a.astype(BF16)
    return high, (a - high.astype(F32)).astype(BF16)


def product(a, b):
    (ah, al), (bh, bl) = a, b
    dot = lambda u, v: jnp.dot(u, v, preferred_element_type=F32)
    return dot(ah, bh) + (dot(ah, bl) + dot(al, bh))


def inverse_of(square):
    size = square.shape[0]
    eye = lax.broadcasted_iota(jnp.int32, (size, size), 0) == lax.broadcasted_iota(
        jnp.int32, (size, size), 1
    )
    diagonal = jnp.where(eye, square, 0.0)
    across = 1.0 / jnp.sum(diagonal, axis=0, keepdims=True)
    down = 1.0 / jnp.sum(diagonal, axis=1, keepdims=True)
    identity = jnp.where(eye, 1.0, 0.0)
    error = identity - square * across
    first = identity + error
    parts = split(error)
    second = product(parts, parts)
    return down * (first + (second + product(parts, split(second))))


def kernel(m_hbm, l_ref, u_ref, m_ref, x_buf, m_sem, send_sem, own_sem, ux_sem, xz_sem, xx_sem, mc_sem, ls_sem,
           ready_x, ready_y, ready_z, ready_w):
    row, col = lax.axis_index("row"), lax.axis_index("col")
    z, x = lax.div(row, NX), lax.rem(row, NX)
    y, core = lax.div(col, 2), lax.rem(col, 2)
    rows, cols = u_ref.shape
    quarter = rows // NX
    chunk = quarter // CHUNKS
    piece = NB // NX
    top = row == 0
    below = row != 0
    first_col = col == 0
    even = core == 0
    mirror = even & (y != 0)
    other_col = col != 0
    root = top & first_col
    bottom = z == 0
    one = lambda cond: jnp.where(cond, 1, 0)

    hub = z == HUB
    chain = other_col & (z <= CHAIN) & (lax.rem(z, 2) == 0)
    source = first_col & bottom
    relay = first_col & (z == 4)
    first_hub = first_col & hub
    other_hub = other_col & hub
    down_u = [(chain, z + 2), (chain, z + 1)] + [(other_hub, to) for to in (12, 14, 11, 15)]
    down_x = [
        ((source | first_hub | relay) if i < 2 else (source | first_hub),
         jnp.where(source, i + 1, jnp.where(relay, 7 + i, to)))
        for i, to in enumerate((9, 14, 10, 15, 11, 12))
    ]
    parent_z = jnp.where(
        first_col,
        jnp.where(z <= NEAR, 0, jnp.where(z < 9, 4, HUB)),
        jnp.where(z > CHAIN + 2, HUB, jnp.where(lax.rem(z, 2) == 0, z - 2, z - 1)),
    )
    children = (jnp.where(source, NEAR, 0) + jnp.where(relay, 2, 0) + jnp.where(first_hub, 6, 0)
                + jnp.where(chain, 2, 0) + jnp.where(other_hub, 4, 0))

    def at_x(j):
        return z * NX + lax.rem(x + j, NX)

    from_root_x = bottom & (x != 0) & first_col
    from_root_y = top & mirror
    from_root_z = (z > 0) & (z <= NEAR) & (x == 0) & first_col
    by_parent = (z > 0) & jnp.logical_not(from_root_z)

    narrow = pltpu.make_async_copy(m_hbm.at[:, pl.ds(0, NB)], m_ref.at[:, pl.ds(0, NB)], m_sem.at[0])
    rest = pl.ds(NB, cols - NB)
    wide = pltpu.make_async_copy(m_hbm.at[:, rest], m_ref.at[:, rest], m_sem.at[1])

    @pl.when(first_col | top)
    def _():
        narrow.start()

    @pl.when(top)
    def _():
        wide.start()

    barrier = pltpu.get_barrier_semaphore()

    usual = jnp.logical_not(root)

    def signal(cond, sem, device):
        one_more = lambda: pl.semaphore_signal(sem, inc=1, device_id=device, device_id_type=MESH)
        one_more() if cond is None else pl.when(cond)(one_more)

    paired = below | (y != 0)
    signal(paired, barrier, (row, y * 2 + 1 - core))
    signal((row == 1) & (col == 1), barrier, (0, 1))
    signal(bottom, barrier, (HUB * NX + x, col))

    @pl.when(usual)
    def _():
        signal(from_root_x | from_root_y | from_root_z, barrier, (0, 0))
        for j in (1, 2, 3):
            signal(x + j < NX, barrier, (row + j, col))
        for cond, to in down_u + down_x:
            signal(cond, barrier, (to * NX + x, col))

    @pl.when(below & first_col)
    def _():
        for k in range(1, NY):
            signal(None, barrier, (row, 2 * k))

    pl.semaphore_wait(
        barrier,
        jnp.where(root, NX - 1 + NEAR + NY - 1,
                  one(paired) + one(top & (col == 1)) + x - one(from_root_x) + one(by_parent)
                  + one(below & mirror)),
    )

    @pl.when(usual)
    def _():
        for j in (1, 2, 3):
            signal((x >= j) & jnp.logical_not(from_root_x & (x == j)), ready_x, (row - j, col))
        signal(by_parent & jnp.logical_not(hub), ready_z, (parent_z * NX + x, col))
        signal(hub, ready_w, (x, col))
        signal(below & mirror, ready_y, (row, 0))

    sections = []
    used = [0]

    def section(cond, body):
        group = []

        def send(part, recv, device, only=None):
            spot = used[0]
            used[0] += 1

            def begin():
                ref = part()
                pltpu.make_async_remote_copy(
                    src_ref=ref, dst_ref=ref, send_sem=send_sem.at[spot], recv_sem=recv,
                    device_id=device, device_id_type=MESH,
                ).start()

            group.append((only, part, spot))
            begin() if only is None else pl.when(only)(begin)

        pl.when(cond)(lambda: body(send))
        sections.append((cond, group))

    def arrived(ref, sem):
        pltpu.make_async_copy(ref, ref, sem).wait()

    def wait_for(cond, sem, count):
        @pl.when(cond)
        def _():
            pl.semaphore_wait(sem, count)

    def x_part(q):
        return x_buf.at[pl.ds(pl.multiple_of(q * piece, piece), piece), :]

    def u_part(q, k, first):
        return u_ref.at[
            pl.ds(pl.multiple_of(q * quarter + k * chunk, chunk), chunk), pl.ds(first, cols - first)
        ]

    def u_quarter(q, first):
        return u_ref.at[pl.ds(pl.multiple_of(q * quarter, quarter), quarter), pl.ds(first, cols - first)]

    def first_part(q, k):
        rows_here = pl.ds(pl.multiple_of(q * quarter + k * (quarter // 2), quarter // 2), quarter // 2)
        return u_ref.at[rows_here, pl.ds(NB, cols - NB)]

    def scatter_u(first):
        def body(send):
            for k in range(CHUNKS):
                for q in (2, 1, 3):
                    send(lambda q=q, k=k: u_part(q, k, first), own_sem.at[k], (q, col))
        return body

    not_back = [at_x(j) != 0 for j in (1, 2, 3)]

    def spread_u(first):
        def body(send):
            for k in range(CHUNKS):
                part = lambda k=k: u_part(x, k, first)

                @pl.when(below)
                def _():
                    arrived(part(), own_sem.at[k])

                for j in (2, 1, 3):
                    send(part, ux_sem.at[j - 1], (at_x(j), col), not_back[j - 1])
                for further, to in down_u:
                    send(part, own_sem.at[k], (to * NX + x, col), further)
        return body

    def late_u(first):
        def body(send):
            for k in range(CHUNKS):
                send(lambda k=k: u_part(x, k, first), own_sem.at[k], (HUB * NX + x, col))
        return body

    @pl.when(first_col | top)
    def _():
        narrow.wait()

    def sent(group):
        for only, part, spot in group:
            gone = lambda part=part, spot=spot: arrived(part(), send_sem.at[spot])
            gone() if only is None else pl.when(only)(gone)

    def flush():
        for cond, group in sections:
            pl.when(cond)(lambda group=group: sent(group))
        sections.clear()

    def start(send):
        x_buf[...] = inverse_of(m_ref[:, :NB])
        for q in (2, 1, 3):
            send(lambda q=q: x_part(q), xz_sem, (q, 0))

    section(root, start)

    @pl.when(top)
    def _():
        wide.wait()
        columns = col * cols + lax.broadcasted_iota(jnp.int32, (rows, cols), 1)
        u_ref[...] = jnp.where(columns < NB, 0.0, m_ref[...]).astype(BF16)
        l_ref[...] = jnp.zeros((rows, NB), BF16)

    columns_here = lambda: m_ref.at[:, pl.ds(0, NB)]

    def to_mirrors(send):
        pl.semaphore_wait(ready_y, NY - 1)
        for k in (4, 5, 3, 6, 2, 7, 1):
            send(columns_here, mc_sem, (row, 2 * k))

    section(first_col & below, to_mirrors)

    wait_for(usual & (x != NX - 1), ready_x, NX - 1 - x)
    wait_for(usual & (children > 0), ready_z, children)

    section(top & other_col, scatter_u(0))
    section(other_col, spread_u(0))

    def last(first):
        def body(send):
            pl.semaphore_wait(ready_w, 1)
            late_u(first)(send)
        return body

    section(bottom & other_col, last(0))

    def finish(first):
        for j in (1, 2, 3):
            arrived(u_quarter(lax.rem(x + NX - j, NX), first), ux_sem.at[j - 1])

    pl.when(below & other_col)(lambda: finish(0))
    later = sections[:2]
    del sections[:2]
    flush()
    sections.extend(later)

    def inverse_rows(send):
        @pl.when(below)
        def _():
            u_ref[:, :NB] = jnp.zeros((rows, NB), BF16)
            arrived(x_part(x), xz_sem)

        mine = lambda: x_part(x)
        for (cond, to), ys in zip(down_x, ((1, 7), (2, 6), (3, 5), (4,), (), ())):
            for k in ys:
                send(mine, xz_sem, (row, 2 * k))
            send(mine, xz_sem, (to * NX + x, 0), cond)
        for j in (2, 1, 3):
            send(mine, xx_sem.at[j - 1], (at_x(j), 0), not_back[j - 1])

    section(first_col, inverse_rows)

    def mirror_rows(send):
        arrived(x_part(x), xz_sem)
        for j in (2, 1, 3):
            send(lambda: x_part(x), xx_sem.at[j - 1], (at_x(j), col), not_back[j - 1])

    section(mirror, mirror_rows)

    def scatter_first(send):
        for k in range(2):
            for q in (2, 1, 3):
                send(lambda q=q, k=k: first_part(q, k), own_sem.at[k], (q, col))

    section(root, scatter_first)

    def to_hub(send):
        pl.semaphore_wait(ready_w, 1)
        send(lambda: x_part(x), xz_sem, (HUB * NX + x, 0))

    section(first_col & bottom, to_hub)

    def spread_first(send):
        for k in range(2):
            @pl.when(below)
            def _():
                arrived(first_part(x, k), own_sem.at[k])

            for j in (2, 1, 3):
                send(lambda k=k: first_part(x, k), ux_sem.at[j - 1], (at_x(j), col), not_back[j - 1])
        for cond, to in down_x + [(bottom, HUB)]:
            for k in range(2):
                send(lambda k=k: first_part(x, k), own_sem.at[k], (to * NX + x, col), cond)

    section(first_col, spread_first)

    def make_lower(send):
        @pl.when(mirror)
        def _():
            arrived(columns_here(), mc_sem)

        left = split(m_ref[:, :NB])
        for j in (1, 2, 3):
            arrived(x_part(lax.rem(x + NX - j, NX)), xx_sem.at[j - 1])
        l_ref[...] = product(left, split(x_buf[...])).astype(BF16)
        send(lambda: l_ref, ls_sem, (row, col + 1))

    section(below & even, make_lower)

    pl.when(below & first_col)(lambda: finish(NB))

    @pl.when(below & (core == 1))
    def _():
        arrived(l_ref, ls_sem)

    flush()


def shards(matrix):
    rows, cols = matrix.shape
    lower, upper = pl.pallas_call(
        kernel,
        out_shape=(jax.ShapeDtypeStruct((rows, NB), BF16), jax.ShapeDtypeStruct((rows, cols), BF16)),
        in_specs=[pl.BlockSpec(memory_space=pl.ANY)],
        out_specs=(pl.BlockSpec(memory_space=pltpu.VMEM), pl.BlockSpec(memory_space=pltpu.VMEM)),
        scratch_shapes=[
            pltpu.VMEM((rows, cols), F32),
            pltpu.VMEM((NB, NB), F32),
            pltpu.SemaphoreType.DMA((2,)),
            pltpu.SemaphoreType.DMA((200,)),
            pltpu.SemaphoreType.DMA((CHUNKS,)),
            pltpu.SemaphoreType.DMA((3,)),
            pltpu.SemaphoreType.DMA,
            pltpu.SemaphoreType.DMA((3,)),
            pltpu.SemaphoreType.DMA,
            pltpu.SemaphoreType.DMA,
        ]
        + [pltpu.SemaphoreType.REGULAR] * 4,
        compiler_params=pltpu.CompilerParams(
            collective_id=0, has_side_effects=True, vmem_limit_bytes=24 * 1024 * 1024
        ),
    )(pltpu.with_memory_space_constraint(matrix, pltpu.HBM))
    return matrix - jnp.dot(lower, upper, preferred_element_type=F32)


def solution(mesh):
    return jax.shard_map(
        shards,
        mesh=mesh,
        in_specs=(P("row", "col"),),
        out_specs=P("row", "col"),
        check_vma=False,
    )
```

```python
import jax
import jax.numpy as jnp
from jax import lax
from jax.experimental import pallas as pl
from jax.experimental.pallas import tpu as pltpu
from jax.sharding import PartitionSpec as P

NB = 256
NX = 4
NZ = 16
NY = 8
CHAIN = 8
HUB = 13
NEAR = 6
CHUNKS = 4
MESH = pl.DeviceIdType.MESH
F32 = jnp.float32
BF16 = jnp.bfloat16


def split(a):
    high = a.astype(BF16)
    return high, (a - high.astype(F32)).astype(BF16)


def product(a, b):
    (ah, al), (bh, bl) = a, b
    dot = lambda u, v: jnp.dot(u, v, preferred_element_type=F32)
    return dot(ah, bh) + (dot(ah, bl) + dot(al, bh))


def inverse_of(square):
    size = square.shape[0]
    eye = lax.broadcasted_iota(jnp.int32, (size, size), 0) == lax.broadcasted_iota(
        jnp.int32, (size, size), 1
    )
    diagonal = jnp.where(eye, square, 0.0)
    across = 1.0 / jnp.sum(diagonal, axis=0, keepdims=True)
    down = 1.0 / jnp.sum(diagonal, axis=1, keepdims=True)
    identity = jnp.where(eye, 1.0, 0.0)
    error = identity - square * across
    first = identity + error
    parts = split(error)
    second = product(parts, parts)
    return down * (first + (second + product(parts, split(second))))


def kernel(m_hbm, l_ref, u_ref, m_ref, x_buf, m_sem, send_sem, own_sem, ux_sem, xz_sem, xx_sem, mc_sem, ls_sem,
           ready_x, ready_y, ready_z, ready_w):
    row, col = lax.axis_index("row"), lax.axis_index("col")
    z, x = lax.div(row, NX), lax.rem(row, NX)
    y, core = lax.div(col, 2), lax.rem(col, 2)
    rows, cols = u_ref.shape
    quarter = rows // NX
    chunk = quarter // CHUNKS
    piece = NB // NX
    top = row == 0
    below = row != 0
    first_col = col == 0
    even = core == 0
    mirror = even & (y != 0)
    other_col = col != 0
    root = top & first_col
    bottom = z == 0
    one = lambda cond: jnp.where(cond, 1, 0)

    hub = z == HUB
    chain = other_col & (z <= CHAIN) & (lax.rem(z, 2) == 0)
    source = first_col & bottom
    relay = first_col & (z == 4)
    first_hub = first_col & hub
    other_hub = other_col & hub
    down_u = [(chain, z + 2), (chain, z + 1)] + [(other_hub, to) for to in (12, 14, 11, 15)]
    down_x = [
        ((source | first_hub | relay) if i < 2 else (source | first_hub),
         jnp.where(source, i + 1, jnp.where(relay, 7 + i, to)))
        for i, to in enumerate((9, 14, 10, 15, 11, 12))
    ]
    parent_z = jnp.where(
        first_col,
        jnp.where(z <= NEAR, 0, jnp.where(z < 9, 4, HUB)),
        jnp.where(z > CHAIN + 2, HUB, jnp.where(lax.rem(z, 2) == 0, z - 2, z - 1)),
    )
    children = (jnp.where(source, NEAR, 0) + jnp.where(relay, 2, 0) + jnp.where(first_hub, 4, 0)
                + jnp.where(chain | other_hub, 2, 0))

    def at_x(j):
        return z * NX + lax.rem(x + j, NX)

    from_root_x = bottom & (x != 0) & first_col
    from_root_y = top & mirror
    from_root_z = (z > 0) & (z <= NEAR) & (x == 0) & first_col
    from_hub = (z == HUB - 1) | (z == HUB - 2)
    by_parent = (z > 0) & jnp.logical_not(from_root_z | from_hub)

    narrow = pltpu.make_async_copy(m_hbm.at[:, pl.ds(0, NB)], m_ref.at[:, pl.ds(0, NB)], m_sem.at[0])
    rest = pl.ds(NB, cols - NB)
    wide = pltpu.make_async_copy(m_hbm.at[:, rest], m_ref.at[:, rest], m_sem.at[1])

    @pl.when(first_col | top)
    def _():
        narrow.start()

    @pl.when(top)
    def _():
        wide.start()

    barrier = pltpu.get_barrier_semaphore()

    usual = jnp.logical_not(root)

    def signal(cond, sem, device):
        one_more = lambda: pl.semaphore_signal(sem, inc=1, device_id=device, device_id_type=MESH)
        one_more() if cond is None else pl.when(cond)(one_more)

    paired = below | (y != 0)
    signal(paired, barrier, (row, y * 2 + 1 - core))
    signal((row == 1) & (col == 1), barrier, (0, 1))
    signal(bottom, barrier, (HUB * NX + x, col))

    @pl.when(usual)
    def _():
        signal(from_root_x | from_root_y | from_root_z, barrier, (0, 0))
        for j in (1, 2, 3):
            signal(x + j < NX, barrier, (row + j, col))
        for cond, to in down_u + down_x:
            nearest = hub & ((to == HUB - 1) | (to == HUB - 2))
            signal(cond & jnp.logical_not(nearest), barrier, (to * NX + x, col))
        signal(from_hub, barrier, (HUB * NX + x, col))

    @pl.when(below & first_col)
    def _():
        for k in range(1, NY):
            signal(None, barrier, (row, 2 * k))

    pl.semaphore_wait(
        barrier,
        jnp.where(root, NX - 1 + NEAR + NY - 1,
                  one(paired) + one(top & (col == 1)) + x - one(from_root_x) + one(by_parent)
                  + one(below & mirror) + jnp.where(hub, 2, 0)),
    )

    @pl.when(usual)
    def _():
        for j in (1, 2, 3):
            signal((x >= j) & jnp.logical_not(from_root_x & (x == j)), ready_x, (row - j, col))
        signal(by_parent & jnp.logical_not(hub), ready_z, (parent_z * NX + x, col))
        signal(hub, ready_w, (x, col))
        signal(below & mirror, ready_y, (row, 0))

    sections = []
    used = [0]

    def section(cond, body):
        group = []

        def send(part, recv, device, only=None):
            spot = used[0]
            used[0] += 1

            def begin():
                ref = part()
                pltpu.make_async_remote_copy(
                    src_ref=ref, dst_ref=ref, send_sem=send_sem.at[spot], recv_sem=recv,
                    device_id=device, device_id_type=MESH,
                ).start()

            group.append((only, part, spot))
            begin() if only is None else pl.when(only)(begin)

        pl.when(cond)(lambda: body(send))
        sections.append((cond, group))

    def arrived(ref, sem):
        pltpu.make_async_copy(ref, ref, sem).wait()

    def wait_for(cond, sem, count):
        @pl.when(cond)
        def _():
            pl.semaphore_wait(sem, count)

    def x_part(q):
        return x_buf.at[pl.ds(pl.multiple_of(q * piece, piece), piece), :]

    def u_part(q, k, first):
        return u_ref.at[
            pl.ds(pl.multiple_of(q * quarter + k * chunk, chunk), chunk), pl.ds(first, cols - first)
        ]

    def u_quarter(q, first):
        return u_ref.at[pl.ds(pl.multiple_of(q * quarter, quarter), quarter), pl.ds(first, cols - first)]

    def first_part(q, k):
        rows_here = pl.ds(pl.multiple_of(q * quarter + k * (quarter // 2), quarter // 2), quarter // 2)
        return u_ref.at[rows_here, pl.ds(NB, cols - NB)]

    def scatter_u(first):
        def body(send):
            for k in range(CHUNKS):
                for q in (2, 1, 3):
                    send(lambda q=q, k=k: u_part(q, k, first), own_sem.at[k], (q, col))
        return body

    over_x = [
        (j, at_x(j), at_x(j) != 0)
        for j in (
            jnp.where(x == 0, 2, NX - x),
            jnp.where((x == 0) | (x == 2), 1, 2),
            jnp.where(x == 1, 1, 3),
        )
    ]

    def spread_u(first):
        def body(send):
            for k in range(CHUNKS):
                part = lambda k=k: u_part(x, k, first)

                @pl.when(below)
                def _():
                    arrived(part(), own_sem.at[k])

                for j, to, allowed in over_x:
                    send(part, ux_sem.at[j - 1], (to, col), allowed)
                for further, to in down_u:
                    send(part, own_sem.at[k], (to * NX + x, col), further)
        return body

    def late_u(first):
        def body(send):
            for k in range(CHUNKS):
                send(lambda k=k: u_part(x, k, first), own_sem.at[k], (HUB * NX + x, col))
        return body

    @pl.when(first_col | top)
    def _():
        narrow.wait()

    def sent(group):
        for only, part, spot in group:
            gone = lambda part=part, spot=spot: arrived(part(), send_sem.at[spot])
            gone() if only is None else pl.when(only)(gone)

    def flush():
        for cond, group in sections:
            pl.when(cond)(lambda group=group: sent(group))
        sections.clear()

    def start(send):
        x_buf[...] = inverse_of(m_ref[:, :NB])
        for q in (2, 1, 3):
            send(lambda q=q: x_part(q), xz_sem, (q, 0))

    section(root, start)

    @pl.when(top)
    def _():
        wide.wait()
        columns = col * cols + lax.broadcasted_iota(jnp.int32, (rows, cols), 1)
        u_ref[...] = jnp.where(columns < NB, 0.0, m_ref[...]).astype(BF16)
        l_ref[...] = jnp.zeros((rows, NB), BF16)

    columns_here = lambda: m_ref.at[:, pl.ds(0, NB)]

    def to_mirrors(send):
        pl.semaphore_wait(ready_y, NY - 1)
        for k in (4, 5, 3, 6, 2, 7, 1):
            send(columns_here, mc_sem, (row, 2 * k))

    section(first_col & below, to_mirrors)

    wait_for(usual & (x != NX - 1), ready_x, NX - 1 - x)
    wait_for(usual & (children > 0), ready_z, children)

    section(top & other_col, scatter_u(0))
    section(other_col, spread_u(0))

    def last(first):
        def body(send):
            pl.semaphore_wait(ready_w, 1)
            late_u(first)(send)
        return body

    section(bottom & other_col, last(0))

    def mirror_rows(send):
        arrived(x_part(x), xz_sem)
        for j, to, allowed in over_x:
            send(lambda: x_part(x), xx_sem.at[j - 1], (to, col), allowed)

    section(mirror, mirror_rows)


    def finish(first):
        for j in (1, 2, 3):
            arrived(u_quarter(lax.rem(x + NX - j, NX), first), ux_sem.at[j - 1])

    pl.when(below & other_col)(lambda: finish(0))
    later = sections[:2]
    del sections[:2]
    flush()
    sections.extend(later)

    def inverse_rows(send):
        @pl.when(below)
        def _():
            u_ref[:, :NB] = jnp.zeros((rows, NB), BF16)
            arrived(x_part(x), xz_sem)

        mine = lambda: x_part(x)
        for (cond, to), ys in zip(down_x, ((1, 7), (2, 6), (3, 5), (4,), (), ())):
            for k in ys:
                send(mine, xz_sem, (row, 2 * k))
            send(mine, xz_sem, (to * NX + x, 0), cond)
        for j, to, allowed in over_x:
            send(mine, xx_sem.at[j - 1], (to, 0), allowed)

    section(first_col, inverse_rows)

    def scatter_first(send):
        for k in range(2):
            for q in (2, 1, 3):
                send(lambda q=q, k=k: first_part(q, k), own_sem.at[k], (q, col))

    section(root, scatter_first)

    def to_hub(send):
        pl.semaphore_wait(ready_w, 1)
        send(lambda: x_part(x), xz_sem, (HUB * NX + x, 0))

    section(first_col & bottom, to_hub)

    def spread_first(send):
        for k in range(2):
            @pl.when(below)
            def _():
                arrived(first_part(x, k), own_sem.at[k])

            for j, to, allowed in over_x:
                send(lambda k=k: first_part(x, k), ux_sem.at[j - 1], (to, col), allowed)
        for cond, to in down_x + [(bottom, HUB)]:
            for k in range(2):
                send(lambda k=k: first_part(x, k), own_sem.at[k], (to * NX + x, col), cond)

    section(first_col, spread_first)

    def make_lower(send):
        @pl.when(mirror)
        def _():
            arrived(columns_here(), mc_sem)

        left = split(m_ref[:, :NB])
        for j in (1, 2, 3):
            arrived(x_part(lax.rem(x + NX - j, NX)), xx_sem.at[j - 1])
        l_ref[...] = product(left, split(x_buf[...])).astype(BF16)
        send(lambda: l_ref, ls_sem, (row, col + 1))

    section(below & even, make_lower)

    pl.when(below & first_col)(lambda: finish(NB))

    @pl.when(below & (core == 1))
    def _():
        arrived(l_ref, ls_sem)

    flush()


def shards(matrix):
    rows, cols = matrix.shape
    lower, upper = pl.pallas_call(
        kernel,
        out_shape=(jax.ShapeDtypeStruct((rows, NB), BF16), jax.ShapeDtypeStruct((rows, cols), BF16)),
        in_specs=[pl.BlockSpec(memory_space=pl.ANY)],
        out_specs=(pl.BlockSpec(memory_space=pltpu.VMEM), pl.BlockSpec(memory_space=pltpu.VMEM)),
        scratch_shapes=[
            pltpu.VMEM((rows, cols), F32),
            pltpu.VMEM((NB, NB), F32),
            pltpu.SemaphoreType.DMA((2,)),
            pltpu.SemaphoreType.DMA((200,)),
            pltpu.SemaphoreType.DMA((CHUNKS,)),
            pltpu.SemaphoreType.DMA((3,)),
            pltpu.SemaphoreType.DMA,
            pltpu.SemaphoreType.DMA((3,)),
            pltpu.SemaphoreType.DMA,
            pltpu.SemaphoreType.DMA,
        ]
        + [pltpu.SemaphoreType.REGULAR] * 4,
        compiler_params=pltpu.CompilerParams(
            collective_id=0, has_side_effects=True, vmem_limit_bytes=24 * 1024 * 1024
        ),
    )(pltpu.with_memory_space_constraint(matrix, pltpu.HBM))
    return matrix - jnp.dot(lower, upper, preferred_element_type=F32)


def solution(mesh):
    return jax.shard_map(
        shards,
        mesh=mesh,
        in_specs=(P("row", "col"),),
        out_specs=P("row", "col"),
        check_vma=False,
    )
```
